512 devices in a mesh: snode: 64 (over z, y), rows: 8 (over x, core).
Axes of the slice: x: 4, y: 8, z: 8, core: 2. Of those that a mesh axis runs over, the one named last changes fastest.
Arguments:
- anc_store: bfloat16 [8192, 8192], P('snode'), may hold values from -9 to 9
- patterns: int32 [64, 8], replicated, may hold values from 0 to 63, all different within a row
- tile_counts: int32 [64], replicated, may hold values from 1 to 8, 448 in all
- tile_owner: int32 [64], replicated, may hold values from 0 to 63, as said below
- l_offdiag: bfloat16 [65536, 512], P(('snode', 'rows')), may hold values from -0.25 to 0.25
- diag_inverse: bfloat16 [32768, 512], P(('snode', 'rows')), may hold values from -1 to 2, as said below
Outputs:
- sigma_offdiag: bfloat16 [65536, 512], P(('snode', 'rows'))
- sigma_diag: float32 [32768, 512], P(('snode', 'rows'))
The draws below stay inside these ranges and needn't reach their ends.
Inputs may be any that keep to these rules, and one draw needn't show every extreme that they name: `patterns`: each supernode's row names 8 different ancestor tiles. Slots before tile_counts[s] of a supernode's pattern are live, the rest padding; some supernode has all 8 slots live. `tile_owner`: a permutation of the ancestor tiles. `diag_inverse`: each supernode's block of 512 rows is lower triangular with diagonal entries between 1 and 2.
All inputs are finite; a program needn't handle non-finite values.
Results may differ from the reference program's by a relative error of at most 0.014.
Values may be sent and summed in bfloat16 or wider, within the bound.
A program may use at most 64 MiB of HBM per device.

```python
import math
import jax
import jax.numpy as jnp
import numpy as np
from jax import lax

W = 512
TILE = 128
K = 8
POOL = 64
SNODES = 64


def owner_table(key):
    return jax.random.permutation(jax.random.fold_in(key, 11), POOL).astype(jnp.int32)


def draw_tile_owner(key, part):
    return owner_table(key)


def draw_anc_store(key, part):
    owner = owner_table(key)
    holder = jnp.zeros((POOL,), jnp.int32).at[owner].set(jnp.arange(POOL, dtype=jnp.int32))
    side_len = POOL * TILE
    noise_key = jax.random.fold_in(key, 12)
    spread = 1.5 / math.sqrt(K * TILE)
    noise = jnp.clip(jax.random.normal(noise_key, (side_len, side_len), jnp.float32), -6.0, 6.0) * spread
    diag_vals = jax.random.uniform(jax.random.fold_in(key, 14), (side_len, 1), jnp.float32, 2.0, 4.0)
    row_index = jnp.arange(side_len, dtype=jnp.int32)
    logical_row = jnp.repeat(holder, TILE) * TILE + row_index % TILE
    col_index = jnp.arange(side_len, dtype=jnp.int32)
    on_diag = logical_row[:, None] == col_index[None, :]
    values = jnp.where(on_diag, diag_vals, noise)
    return values.astype(jnp.bfloat16)


def draw_diag_inverse(key, part):
    total_rows = SNODES * W
    inner = (jnp.arange(total_rows, dtype=jnp.int32) % W)[:, None]
    columns = jnp.arange(W, dtype=jnp.int32)[None, :]
    noise_key = jax.random.fold_in(key, 21)
    noise = jnp.clip(jax.random.normal(noise_key, (total_rows, W), jnp.float32), -1.4, 1.4)
    noise = noise * (0.7 / math.sqrt(W))
    diag_vals = jax.random.uniform(jax.random.fold_in(key, 22), (total_rows, 1), jnp.float32, 1.0, 2.0)
    lower = jnp.where(columns < inner, noise, jnp.zeros_like(noise))
    values = jnp.where(columns == inner, diag_vals, lower)
    return values.astype(jnp.bfloat16)


def block_scale(stream_key, dims, pieces, smallest, high):
    def one(position, parts):
        draws = jax.random.uniform(jax.random.fold_in(jax.random.fold_in(stream_key, 6), position), (parts,), jnp.float32, smallest / len(pieces), high / len(pieces))
        return jnp.repeat(jnp.exp(draws), dims[position] // parts).reshape((-1,) + (1,) * (len(dims) - position - 1))

    loudness = one(*pieces[0])
    for cut in pieces[1:]:
        loudness = loudness * one(*cut)
    return loudness


def distinct(stream_key, rows, number_of, top, lift):
    order = jax.random.permutation(jax.random.fold_in(stream_key, 1), number_of)
    boost = order
    for power in range(3):
        boost = boost * boost // number_of
    boost = boost * lift // number_of
    chance = jax.random.randint(jax.random.fold_in(stream_key, 2), (rows, number_of), 0, 4096) + boost
    sure = jax.random.permutation(jax.random.fold_in(stream_key, 3), rows)[jnp.arange(number_of) % rows]
    chance = jnp.where(jnp.arange(rows)[:, None] == sure[None, :], 1 << 14, chance)
    score = chance * number_of + jnp.arange(number_of)
    return lax.top_k(score.astype(jnp.int32), top)[1].astype(jnp.int32)


def length_profile(count, total, reach, slope):
    weights = [(1 << 20) // math.isqrt(grade ** slope) + 1 for grade in range(2, count + 1)]
    rest, holding = total - reach - (count - 1), [1] * (count - 1)
    while rest > 0:
        free = [i for i in range(count - 1) if holding[i] < reach]
        whole, budget = sum([weights[i] for i in free]), rest
        for i in free:
            addition = min(reach - holding[i], max(1, budget * weights[i] // whole), rest)
            holding[i] = holding[i] + addition
            rest = rest - addition
    return np.array([reach] + holding)


def uneven(rng, number_of, total, bound, slope):
    if number_of == 2:
        one = jax.random.randint(rng, (), max(1, total - bound), min(bound, total - 1) + 1)
        return jnp.stack([one, total - one])
    lengths = jnp.asarray(length_profile(number_of, total, bound, slope), jnp.int32)
    twos = (number_of - 1) // 2
    giver, receiver = lengths[1:1 + 2 * twos:2], lengths[2:2 + 2 * twos:2]
    slack = jnp.minimum(giver - 1, bound - receiver)
    moved = jax.random.randint(jax.random.fold_in(rng, 1), (twos,), 0, 1 << 20) % (slack + 1)
    lengths = lengths.at[1:1 + 2 * twos:2].set(giver - moved).at[2:2 + 2 * twos:2].set(receiver + moved)
    return lengths[jax.random.permutation(jax.random.fold_in(rng, 2), number_of)]


def bell_draw(rng, dims, scale, limit, split=(), kind=jnp.bfloat16):
    entries = jax.random.normal(rng, dims, jnp.float32) * scale
    if len(split) > 0:
        entries = block_scale(rng, dims, split, -0.22, 0.18) * entries
    return jnp.clip(entries, min=-limit, max=limit).astype(kind)


def setup_inputs(seed: int = 0) -> dict:
    streams_of = jax.random.split(jax.random.key(seed), 7)
    anc_store = draw_anc_store(jax.random.fold_in(streams_of[6], 71), 0)
    patterns = distinct(streams_of[1], SNODES, POOL, K, 1024)
    tile_counts = uneven(streams_of[2], SNODES, SNODES * K * 7 // 8, K, 2).astype(jnp.int32)
    tile_owner = draw_tile_owner(jax.random.fold_in(streams_of[6], 71), 0)
    l_offdiag = bell_draw(streams_of[4], (SNODES * K * TILE, W), (K * TILE // 2) ** -0.5, 0.25, ((0, 512),))
    diag_inverse = draw_diag_inverse(jax.random.fold_in(streams_of[6], 71), 0)
    return {"anc_store": anc_store, "patterns": patterns, "tile_counts": tile_counts, "tile_owner": tile_owner, "l_offdiag": l_offdiag, "diag_inverse": diag_inverse}


def reference(anc_store, patterns, tile_counts, tile_owner, l_offdiag, diag_inverse):
    blocks = anc_store.reshape(POOL, TILE, POOL, TILE)
    live_mask = jnp.arange(K, dtype=jnp.int32)[None, :] < tile_counts[:, None]

    def per_group(group):
        pattern = lax.dynamic_index_in_dim(patterns, group, 0, keepdims=False)
        keep = lax.dynamic_index_in_dim(live_mask, group, 0, keepdims=False)
        holders = jnp.take(tile_owner, pattern, axis=0)
        row_tiles = jnp.take(blocks, holders, axis=0)
        ancestor = jnp.take(row_tiles, pattern, axis=2)
        both_live = keep[:, None, None, None] & keep[None, None, :, None]
        ancestor = jnp.where(both_live, ancestor, jnp.zeros_like(ancestor))
        ancestor = ancestor.reshape(K * TILE, K * TILE)
        l_block = lax.dynamic_slice_in_dim(l_offdiag, group * (K * TILE), K * TILE, 0)
        keep_rows = jnp.repeat(keep, TILE)
        l_block = jnp.where(keep_rows[:, None], l_block, jnp.zeros_like(l_block))
        inverse_block = lax.dynamic_slice_in_dim(diag_inverse, group * W, W, 0)
        u_factor = jnp.dot(l_block, inverse_block, preferred_element_type=jnp.float32).astype(jnp.bfloat16)
        y_block = jnp.dot(ancestor, u_factor, preferred_element_type=jnp.float32)
        offdiag = (-y_block).astype(jnp.bfloat16)
        base_diag = jnp.dot(inverse_block.T, inverse_block, preferred_element_type=jnp.float32)
        update = jnp.dot(u_factor.T, offdiag, preferred_element_type=jnp.float32)
        return offdiag, base_diag - update

    offdiag_all, diag_all = lax.map(per_group, jnp.arange(SNODES, dtype=jnp.int32))
    return offdiag_all.reshape(SNODES * K * TILE, W), diag_all.reshape(SNODES * W, W)
```

```python
import functools

import jax
import jax.numpy as jnp
from jax import lax
from jax.experimental import pallas as pl
from jax.experimental.pallas import tpu as pltpu
from jax.sharding import PartitionSpec as P

MESH = pl.DeviceIdType.MESH
VMEM = pl.BlockSpec(memory_space=pltpu.VMEM)


def pick_kernel(count, tile, cols_ref, store_ref, out_ref, sem):
    def start(i, carry):
        col = pl.multiple_of(cols_ref[i] * tile, tile)
        pltpu.make_async_copy(store_ref.at[:, pl.ds(col, tile)], out_ref.at[i], sem).start()
        return carry

    lax.fori_loop(0, count, start, 0)
    pltpu.make_async_copy(out_ref, out_ref, sem).wait()


def pick_tiles(store, cols, tile):
    count = cols.shape[0]
    return pl.pallas_call(
        functools.partial(pick_kernel, count, tile),
        out_shape=jax.ShapeDtypeStruct((count, store.shape[0], tile), store.dtype),
        in_specs=[pl.BlockSpec(memory_space=pltpu.SMEM), pl.BlockSpec(memory_space=pl.ANY)],
        out_specs=VMEM,
        scratch_shapes=[pltpu.SemaphoreType.DMA],
        name="pick_tiles",
    )(cols, store)


def greet(n):
    snode, me = lax.axis_index("snode"), lax.axis_index("rows")
    barrier = pltpu.get_barrier_semaphore()
    for step in range(1, n):
        pl.semaphore_signal(
            barrier, inc=1, device_id=(snode, lax.rem(me + step, n)), device_id_type=MESH
        )
    pl.semaphore_wait(barrier, n - 1)


def exchange(n, gather, src_ref, dst_ref, send_sem, recv_sem, local_sem):
    snode, me = lax.axis_index("snode"), lax.axis_index("rows")
    greet(n)
    copies = []
    for step in range(1, n):
        peer = lax.rem(me + step, n)
        copy = pltpu.make_async_remote_copy(
            src_ref=src_ref if gather else src_ref.at[peer],
            dst_ref=dst_ref.at[me],
            send_sem=send_sem.at[step - 1],
            recv_sem=recv_sem.at[step - 1],
            device_id=(snode, peer),
            device_id_type=MESH,
        )
        copy.start()
        copies.append(copy)
    own = pltpu.make_async_copy(
        src_ref if gather else src_ref.at[me], dst_ref.at[me], local_sem
    )
    own.start()
    own.wait()
    for copy in copies:
        copy.wait()


def sems(n):
    return [
        pltpu.SemaphoreType.DMA((n - 1,)),
        pltpu.SemaphoreType.DMA((n - 1,)),
        pltpu.SemaphoreType.DMA,
    ]


def gather_kernel(n, x_ref, o_ref, *semaphores):
    exchange(n, True, x_ref, o_ref, *semaphores)


def gather_rows(x, n, collective_id, name):
    return pl.pallas_call(
        functools.partial(gather_kernel, n),
        out_shape=jax.ShapeDtypeStruct((n,) + x.shape, x.dtype),
        in_specs=[VMEM],
        out_specs=VMEM,
        scratch_shapes=sems(n),
        compiler_params=pltpu.CompilerParams(collective_id=collective_id, has_side_effects=True),
        name=name,
    )(x)


def product_kernel(n, tiles_ref, u_ref, own_u_ref, live_ref, y_ref, part_ref, held, *semaphores):
    exchange(n, False, tiles_ref, held, *semaphores)
    total = jnp.zeros(y_ref.shape, jnp.float32)
    for m in range(n):
        total += jnp.dot(held[m], u_ref[m], preferred_element_type=jnp.float32)
    y = (-(total * live_ref[...])).astype(y_ref.dtype)
    y_ref[...] = y
    part = lax.dot_general(
        own_u_ref[...], y, (((0,), (0,)), ((), ())), preferred_element_type=jnp.float32
    )
    part_ref[...] = part.astype(part_ref.dtype).reshape(part_ref.shape)


def product(tiles, u_all, own_u, live, n, collective_id):
    width = own_u.shape[1]
    return pl.pallas_call(
        functools.partial(product_kernel, n),
        out_shape=(
            jax.ShapeDtypeStruct(own_u.shape, jnp.bfloat16),
            jax.ShapeDtypeStruct((n, width // n, width), jnp.bfloat16),
        ),
        in_specs=[VMEM] * 4,
        out_specs=(VMEM, VMEM),
        scratch_shapes=[pltpu.VMEM(tiles.shape, tiles.dtype)] + sems(n),
        compiler_params=pltpu.CompilerParams(collective_id=collective_id, has_side_effects=True),
        name="product",
    )(tiles, u_all, own_u, live)


def update_kernel(n, part_ref, base_ref, o_ref, held, *semaphores):
    exchange(n, False, part_ref, held, *semaphores)
    total = base_ref[...]
    for m in range(n):
        total -= held[m].astype(jnp.float32)
    o_ref[...] = total


def update(part, base, n, collective_id):
    return pl.pallas_call(
        functools.partial(update_kernel, n),
        out_shape=jax.ShapeDtypeStruct(base.shape, jnp.float32),
        in_specs=[VMEM] * 2,
        out_specs=VMEM,
        scratch_shapes=[pltpu.VMEM(part.shape, part.dtype)] + sems(n),
        compiler_params=pltpu.CompilerParams(collective_id=collective_id, has_side_effects=True),
        name="update",
    )(part, base)


def per_device(n, anc_store, patterns, tile_counts, tile_owner, l_offdiag, diag_inverse):
    tile = anc_store.shape[0]
    width = diag_inverse.shape[1]
    band = diag_inverse.shape[0]
    group = lax.axis_index("snode")
    part = lax.axis_index("rows")
    cols = lax.dynamic_slice_in_dim(patterns, part, 1, 1)[:, 0]
    outgoing = pick_tiles(anc_store, cols, tile)
    incoming = lax.all_to_all(outgoing, "snode", split_axis=0, concat_axis=0, tiled=True)

    own_live = part < lax.dynamic_index_in_dim(tile_counts, group, 0, keepdims=False)
    piece = gather_rows(diag_inverse, n, 1, "gather_diag").reshape(width, width)
    masked_l = jnp.where(own_live, l_offdiag, jnp.zeros_like(l_offdiag))
    own_u = jnp.dot(masked_l, piece, preferred_element_type=jnp.float32).astype(jnp.bfloat16)
    u_all = gather_rows(own_u, n, 2, "gather_u")
    own_cols = lax.dynamic_slice_in_dim(piece, part * band, band, 1)
    base = lax.dot_general(
        own_cols, piece, (((0,), (0,)), ((), ())), preferred_element_type=jnp.float32
    )

    own_pattern = lax.dynamic_index_in_dim(patterns, group, 0, keepdims=False)
    sources = jnp.take(tile_owner, own_pattern, axis=0, mode="clip")
    arranged = jnp.take(incoming, sources, axis=0, mode="clip")
    live = jnp.broadcast_to(own_live.astype(jnp.float32), (1, width))
    offdiag, parts = product(arranged, u_all, own_u, live, n, 3)
    return offdiag, update(parts, base, n, 4)


def solution(mesh):
    in_specs = (
        P("snode", None),
        P(),
        P(),
        P(),
        P(("snode", "rows"), None),
        P(("snode", "rows"), None),
    )
    out_specs = (P(("snode", "rows"), None), P(("snode", "rows"), None))
    return jax.shard_map(
        functools.partial(per_device, mesh.shape["rows"]),
        mesh=mesh,
        in_specs=in_specs,
        out_specs=out_specs,
        check_vma=False,
    )
```

```python
import functools

import jax
import jax.numpy as jnp
from jax import lax
from jax.experimental import pallas as pl
from jax.experimental.pallas import tpu as pltpu
from jax.sharding import PartitionSpec as P

LANES = 128
MESH = pl.DeviceIdType.MESH
VMEM = pl.BlockSpec(memory_space=pltpu.VMEM)


def pick_kernel(count, tile, cols_ref, store_ref, out_ref, sem):
    def start(i, carry):
        col = pl.multiple_of(cols_ref[i] * tile, tile)
        pltpu.make_async_copy(store_ref.at[:, pl.ds(col, tile)], out_ref.at[i], sem).start()
        return carry

    lax.fori_loop(0, count, start, 0)
    pltpu.make_async_copy(out_ref, out_ref, sem).wait()


def pick_tiles(store, cols, tile):
    count = cols.shape[0]
    return pl.pallas_call(
        functools.partial(pick_kernel, count, tile),
        out_shape=jax.ShapeDtypeStruct((count, store.shape[0], tile), store.dtype),
        in_specs=[pl.BlockSpec(memory_space=pltpu.SMEM), pl.BlockSpec(memory_space=pl.ANY)],
        out_specs=VMEM,
        scratch_shapes=[pltpu.SemaphoreType.DMA],
        name="pick_tiles",
    )(cols, store)


def level_kernel(
    n, count, side,
    src_ref, out_tiles, l_ref, diag_ref, live_ref,
    y_ref, parts_ref, base_ref,
    pool, diag_all, u_all, stage, tiles, parts, wide, total,
    pool_send, pool_recv, row_send, row_recv, local_sem,
):
    snode, me = lax.axis_index("snode"), lax.axis_index("rows")
    major, minor = snode // side, lax.rem(snode, side)

    def other(step):
        shift = lax.rem(step * 27, count)
        to_major = lax.rem(major + shift // side, count // side)
        to_minor = lax.rem(minor + lax.rem(shift, side), side)
        return to_major * side + to_minor

    def greet_other(step, carry):
        pl.semaphore_signal(barrier, inc=1, device_id=(other(step), me), device_id_type=MESH)
        return carry

    barrier = pltpu.get_barrier_semaphore()
    for step in range(1, n):
        pl.semaphore_signal(
            barrier, inc=1, device_id=(snode, lax.rem(me + step, n)), device_id_type=MESH
        )
    lax.fori_loop(1, count, greet_other, 0)
    pl.semaphore_wait(barrier, n + count - 2)

    def row_copies(phase, src_of, dst):
        copies = []
        for step in range(1, n):
            peer = lax.rem(me + step, n)
            copy = pltpu.make_async_remote_copy(
                src_ref=src_of(peer),
                dst_ref=dst.at[me],
                send_sem=row_send.at[phase, step - 1],
                recv_sem=row_recv.at[phase, step - 1],
                device_id=(snode, peer),
                device_id_type=MESH,
            )
            copy.start()
            copies.append(copy)
        return copies

    def pool_copy(step):
        peer = other(step)
        return pltpu.make_async_remote_copy(
            src_ref=out_tiles.at[peer],
            dst_ref=pool.at[snode],
            send_sem=pool_send.at[step],
            recv_sem=pool_recv.at[step],
            device_id=(peer, me),
            device_id_type=MESH,
        )

    def start_pool(step, carry):
        pool_copy(step).start()
        return carry

    def wait_pool(step, carry):
        pool_copy(step).wait()
        return carry

    diag_copies = row_copies(0, lambda peer: diag_ref, diag_all)
    lax.fori_loop(1, count, start_pool, 0)
    own_diag = pltpu.make_async_copy(diag_ref, diag_all.at[me], local_sem.at[0])
    own_diag.start()
    own_tile = pltpu.make_async_copy(out_tiles.at[snode], pool.at[snode], local_sem.at[1])
    own_tile.start()
    own_diag.wait()
    for copy in diag_copies:
        copy.wait()

    band, width = diag_ref.shape
    depth = l_ref.shape[0]
    piece = diag_all[...].reshape(width, width)
    u_all[me] = jnp.dot(l_ref[...], piece, preferred_element_type=jnp.float32).astype(u_all.dtype)
    per_block = LANES // band
    start = pl.multiple_of(me // per_block * LANES, LANES)
    columns = diag_all[:, :, pl.ds(start, LANES)].reshape(width, LANES)
    wide[...] = lax.dot_general(
        columns, piece, (((0,), (0,)), ((), ())), preferred_element_type=jnp.float32
    )
    row = pl.multiple_of(lax.rem(me, per_block) * band, band)
    base_ref[...] = wide[pl.ds(row, band), :]
    u_copies = row_copies(1, lambda peer: u_all.at[me], u_all)
    for copy in u_copies:
        copy.wait()
    own_tile.wait()
    lax.fori_loop(1, count, wait_pool, 0)

    for k in range(n):
        stage[k] = pool[src_ref[k]]
    tile_copies = row_copies(2, lambda peer: stage.at[peer], tiles)
    total[...] = jnp.dot(stage[me], u_all[me], preferred_element_type=jnp.float32)
    for step, copy in enumerate(tile_copies):
        copy.wait()
        origin = lax.rem(me + n - 1 - step, n)
        total[...] += jnp.dot(tiles[origin], u_all[origin], preferred_element_type=jnp.float32)
    y = (-(total[...] * live_ref[...])).astype(y_ref.dtype)
    part = lax.dot_general(
        u_all[me], y, (((0,), (0,)), ((), ())), preferred_element_type=jnp.float32
    )
    parts[...] = part.astype(parts.dtype).reshape(parts.shape)
    y_ref[...] = y
    part_copies = row_copies(3, lambda peer: parts.at[peer], parts_ref)
    own_part = pltpu.make_async_copy(parts.at[me], parts_ref.at[me], local_sem.at[2])
    own_part.start()
    own_part.wait()
    for copy in part_copies:
        copy.wait()


def level(sources, outgoing, masked_l, diag, live, n, side):
    count, tile, _ = outgoing.shape
    band, width = diag.shape
    bf16 = jnp.bfloat16
    return pl.pallas_call(
        functools.partial(level_kernel, n, count, side),
        out_shape=(
            jax.ShapeDtypeStruct((tile, width), bf16),
            jax.ShapeDtypeStruct((n, band, width), bf16),
            jax.ShapeDtypeStruct((band, width), jnp.float32),
        ),
        in_specs=[pl.BlockSpec(memory_space=pltpu.SMEM)] + [VMEM] * 4,
        out_specs=(VMEM,) * 3,
        scratch_shapes=[
            pltpu.VMEM((count, tile, tile), bf16),
            pltpu.VMEM((n, band, width), bf16),
            pltpu.VMEM((n, tile, width), bf16),
            pltpu.VMEM((n, tile, tile), bf16),
            pltpu.VMEM((n, tile, tile), bf16),
            pltpu.VMEM((n, band, width), bf16),
            pltpu.VMEM((LANES, width), jnp.float32),
            pltpu.VMEM((tile, width), jnp.float32),
            pltpu.SemaphoreType.DMA((count,)),
            pltpu.SemaphoreType.DMA((count,)),
            pltpu.SemaphoreType.DMA((4, n - 1)),
            pltpu.SemaphoreType.DMA((4, n - 1)),
            pltpu.SemaphoreType.DMA((3,)),
        ],
        compiler_params=pltpu.CompilerParams(collective_id=1, has_side_effects=True),
        name="level",
    )(sources, outgoing, masked_l, diag, live)


def finish_kernel(y_ref, parts_ref, base_ref, off_ref, diag_ref):
    off_ref[...] = y_ref[...]
    total = base_ref[...]
    for m in range(parts_ref.shape[0]):
        total -= parts_ref[m].astype(jnp.float32)
    diag_ref[...] = total


def finish(y, parts, base):
    return pl.pallas_call(
        finish_kernel,
        out_shape=(
            jax.ShapeDtypeStruct(y.shape, y.dtype),
            jax.ShapeDtypeStruct(base.shape, base.dtype),
        ),
        in_specs=[VMEM] * 3,
        out_specs=(VMEM, VMEM),
        name="finish",
    )(y, parts, base)


def per_device(n, side, anc_store, patterns, tile_counts, tile_owner, l_offdiag, diag_inverse):
    tile = anc_store.shape[0]
    width = diag_inverse.shape[1]
    group = lax.axis_index("snode")
    part = lax.axis_index("rows")
    cols = lax.dynamic_slice_in_dim(patterns, part, 1, 1)[:, 0]
    outgoing = pick_tiles(anc_store, cols, tile)
    own_live = part < lax.dynamic_index_in_dim(tile_counts, group, 0, keepdims=False)
    masked_l = jnp.where(own_live, l_offdiag, jnp.zeros_like(l_offdiag))
    own_pattern = lax.dynamic_index_in_dim(patterns, group, 0, keepdims=False)
    pool_ids = jnp.arange(tile_owner.shape[0], dtype=jnp.int32)
    hit = own_pattern[:, None] == pool_ids[None, :]
    sources = jnp.sum(jnp.where(hit, tile_owner[None, :], 0), axis=1)
    live = jnp.broadcast_to(own_live.astype(jnp.float32), (1, width))
    return finish(*level(sources, outgoing, masked_l, diag_inverse, live, n, side))


def solution(mesh):
    in_specs = (
        P("snode", None),
        P(),
        P(),
        P(),
        P(("snode", "rows"), None),
        P(("snode", "rows"), None),
    )
    out_specs = (P(("snode", "rows"), None), P(("snode", "rows"), None))
    return jax.shard_map(
        functools.partial(per_device, mesh.shape["rows"], 8),
        mesh=mesh,
        in_specs=in_specs,
        out_specs=out_specs,
        check_vma=False,
    )
```

```python
import functools

import jax
import jax.numpy as jnp
from jax import lax
from jax.experimental import pallas as pl
from jax.experimental.pallas import tpu as pltpu
from jax.sharding import PartitionSpec as P

LANES = 128
MESH = pl.DeviceIdType.MESH
VMEM = pl.BlockSpec(memory_space=pltpu.VMEM)


ORDER = (3, 5, 2, 6, 1, 7, 4)


def pick_kernel(
    tile, patterns_ref, counts_ref, owner_ref, store_ref, l_ref,
    out_ref, src_ref, masked_ref, live_ref, sem,
):
    group, part = lax.axis_index("snode"), lax.axis_index("rows")
    majors, minors = out_ref.shape[:2]

    def start(i, carry):
        col = pl.multiple_of(patterns_ref[part, i] * tile, tile)
        pltpu.make_async_copy(
            store_ref.at[:, pl.ds(col, tile)], out_ref.at[i // minors, lax.rem(i, minors)], sem
        ).start()
        return carry

    lax.fori_loop(0, majors * minors, start, 0)
    slots = patterns_ref.shape[0]
    for k in range(slots):
        owner = owner_ref[patterns_ref[k, group]]
        src_ref[k] = owner
        src_ref[slots + k] = lax.rem(owner, minors) * majors + owner // minors
    live = (part < counts_ref[group]).astype(jnp.float32)
    keep = jnp.full(live_ref.shape, live, jnp.float32)
    live_ref[...] = keep
    loaded = l_ref[...]
    masked_ref[...] = jnp.where(keep > 0, loaded, jnp.zeros_like(loaded))
    pltpu.make_async_copy(out_ref, out_ref, sem).wait()


def pick_tiles(patterns, counts, owner, store, l_offdiag, side):
    tile = store.shape[0]
    smem = pl.BlockSpec(memory_space=pltpu.SMEM)
    return pl.pallas_call(
        functools.partial(pick_kernel, tile),
        out_shape=(
            jax.ShapeDtypeStruct((owner.shape[0] // side, side, tile, tile), store.dtype),
            jax.ShapeDtypeStruct((2 * patterns.shape[0],), jnp.int32),
            jax.ShapeDtypeStruct(l_offdiag.shape, l_offdiag.dtype),
            jax.ShapeDtypeStruct((1, l_offdiag.shape[1]), jnp.float32),
        ),
        in_specs=[smem] * 3 + [pl.BlockSpec(memory_space=pl.ANY), VMEM],
        out_specs=(VMEM, smem, VMEM, VMEM),
        scratch_shapes=[pltpu.SemaphoreType.DMA],
        name="pick_tiles",
    )(patterns, counts, owner, store, l_offdiag)


def level_kernel(
    n, src_ref, out_tiles, l_ref, diag_ref, live_ref,
    y_ref, parts_ref, base_ref,
    top_mid, low_mid, top_pool, low_pool, diag_all, u_all, stage, tiles, parts, wide, total,
    pool_send, pool_recv, row_send, row_recv, local_sem,
):
    snode, me = lax.axis_index("snode"), lax.axis_index("rows")
    majors, minors, tile, _ = out_tiles.shape
    half = tile // 2
    major, minor = snode // minors, lax.rem(snode, minors)

    barrier = pltpu.get_barrier_semaphore()
    for step in range(1, n):
        pl.semaphore_signal(
            barrier, inc=1, device_id=(snode, lax.rem(me + step, n)), device_id_type=MESH
        )
    for step in ORDER:
        for peer in (
            major * minors + lax.rem(minor + step, minors),
            lax.rem(major + step, majors) * minors + minor,
        ):
            pl.semaphore_signal(barrier, inc=1, device_id=(peer, me), device_id_type=MESH)
    pl.semaphore_wait(barrier, n - 1 + 2 * len(ORDER))

    def row_copies(phase, src_of, dst):
        copies = []
        for step in range(1, n):
            peer = lax.rem(me + step, n)
            copy = pltpu.make_async_remote_copy(
                src_ref=src_of(peer),
                dst_ref=dst.at[me],
                send_sem=row_send.at[phase, step - 1],
                recv_sem=row_recv.at[phase, step - 1],
                device_id=(snode, peer),
                device_id_type=MESH,
            )
            copy.start()
            copies.append(copy)
        return copies

    def pool_copies(phase, top_src, top_dst, low_src, low_dst):
        copies = []
        for step in ORDER:
            to_minor, to_major = lax.rem(minor + step, minors), lax.rem(major + step, majors)
            along_minor = (to_minor, (major * minors + to_minor, me))
            along_major = (to_major, (to_major * minors + minor, me))
            first, second = (along_minor, along_major) if phase == 0 else (along_major, along_minor)
            for lane, src, dst, (index, device) in (
                (2 * phase, top_src, top_dst, first),
                (2 * phase + 1, low_src, low_dst, second),
            ):
                copy = pltpu.make_async_remote_copy(
                    src_ref=src(index),
                    dst_ref=dst,
                    send_sem=pool_send.at[lane, step - 1],
                    recv_sem=pool_recv.at[lane, step - 1],
                    device_id=device,
                    device_id_type=MESH,
                )
                copy.start()
                copies.append(copy)
        return copies

    def local(slot, src, dst):
        copy = pltpu.make_async_copy(src, dst, local_sem.at[slot])
        copy.start()
        return copy

    top_out = lambda to: out_tiles.at[:, to, pl.ds(0, half)]
    low_out = lambda to: out_tiles.at[to, :, pl.ds(half, half)]
    diag_copies = row_copies(0, lambda peer: diag_ref, diag_all)
    first = pool_copies(0, top_out, top_mid.at[minor], low_out, low_mid.at[major])
    own_diag = local(0, diag_ref, diag_all.at[me])
    own_top = local(1, top_out(minor), top_mid.at[minor])
    own_low = local(2, low_out(major), low_mid.at[major])
    own_diag.wait()
    for copy in diag_copies:
        copy.wait()

    band, width = diag_ref.shape
    depth = l_ref.shape[0]
    piece = diag_all[...].reshape(width, width)
    u_all[me] = jnp.dot(l_ref[...], piece, preferred_element_type=jnp.float32).astype(u_all.dtype)
    per_block = LANES // band
    start = pl.multiple_of(me // per_block * LANES, LANES)
    columns = diag_all[:, :, pl.ds(start, LANES)].reshape(width, LANES)
    wide[...] = lax.dot_general(
        columns, piece, (((0,), (0,)), ((), ())), preferred_element_type=jnp.float32
    )
    row = pl.multiple_of(lax.rem(me, per_block) * band, band)
    base_ref[...] = wide[pl.ds(row, band), :]
    u_copies = row_copies(1, lambda peer: u_all.at[me], u_all)
    own_top.wait()
    own_low.wait()
    for copy in first:
        copy.wait()
    top_via = lambda to: top_mid.at[:, to]
    low_via = lambda to: low_mid.at[:, to]
    second = pool_copies(1, top_via, top_pool.at[major], low_via, low_pool.at[minor])
    end_top = local(3, top_via(major), top_pool.at[major])
    end_low = local(4, low_via(minor), low_pool.at[minor])
    for copy in u_copies:
        copy.wait()
    end_top.wait()
    end_low.wait()
    for copy in second:
        copy.wait()

    for k in range(n):
        top, low = src_ref[k], src_ref[n + k]
        stage[k, :half] = top_pool[top // minors, lax.rem(top, minors)]
        stage[k, half:] = low_pool[low // majors, lax.rem(low, majors)]
    tile_copies = row_copies(2, lambda peer: stage.at[peer], tiles)
    total[...] = jnp.dot(stage[me], u_all[me], preferred_element_type=jnp.float32)
    for step, copy in enumerate(tile_copies):
        copy.wait()
        origin = lax.rem(me + n - 1 - step, n)
        total[...] += jnp.dot(tiles[origin], u_all[origin], preferred_element_type=jnp.float32)
    y = (-(total[...] * live_ref[...])).astype(y_ref.dtype)
    part = lax.dot_general(
        u_all[me], y, (((0,), (0,)), ((), ())), preferred_element_type=jnp.float32
    )
    parts[...] = part.astype(parts.dtype).reshape(parts.shape)
    y_ref[...] = y
    part_copies = row_copies(3, lambda peer: parts.at[peer], parts_ref)
    local(5, parts.at[me], parts_ref.at[me]).wait()
    for copy in part_copies:
        copy.wait()


def level(outgoing, sources, masked_l, live, diag, n):
    majors, minors, tile, _ = outgoing.shape
    band, width = diag.shape
    bf16 = jnp.bfloat16
    return pl.pallas_call(
        functools.partial(level_kernel, n),
        out_shape=(
            jax.ShapeDtypeStruct((tile, width), bf16),
            jax.ShapeDtypeStruct((n, band, width), bf16),
            jax.ShapeDtypeStruct((band, width), jnp.float32),
        ),
        in_specs=[pl.BlockSpec(memory_space=pltpu.SMEM)] + [VMEM] * 4,
        out_specs=(VMEM,) * 3,
        scratch_shapes=[
            pltpu.VMEM((minors, majors, tile // 2, tile), bf16),
            pltpu.VMEM((majors, minors, tile // 2, tile), bf16),
            pltpu.VMEM((majors, minors, tile // 2, tile), bf16),
            pltpu.VMEM((minors, majors, tile // 2, tile), bf16),
            pltpu.VMEM((n, band, width), bf16),
            pltpu.VMEM((n, tile, width), bf16),
            pltpu.VMEM((n, tile, tile), bf16),
            pltpu.VMEM((n, tile, tile), bf16),
            pltpu.VMEM((n, band, width), bf16),
            pltpu.VMEM((LANES, width), jnp.float32),
            pltpu.VMEM((tile, width), jnp.float32),
            pltpu.SemaphoreType.DMA((4, len(ORDER))),
            pltpu.SemaphoreType.DMA((4, len(ORDER))),
            pltpu.SemaphoreType.DMA((4, n - 1)),
            pltpu.SemaphoreType.DMA((4, n - 1)),
            pltpu.SemaphoreType.DMA((6,)),
        ],
        compiler_params=pltpu.CompilerParams(collective_id=1, has_side_effects=True),
        name="level",
    )(sources, outgoing, masked_l, diag, live)


def finish_kernel(y_ref, parts_ref, base_ref, off_ref, diag_ref):
    off_ref[...] = y_ref[...]
    total = base_ref[...]
    for m in range(parts_ref.shape[0]):
        total -= parts_ref[m].astype(jnp.float32)
    diag_ref[...] = total


def finish(y, parts, base):
    return pl.pallas_call(
        finish_kernel,
        out_shape=(
            jax.ShapeDtypeStruct(y.shape, y.dtype),
            jax.ShapeDtypeStruct(base.shape, base.dtype),
        ),
        in_specs=[VMEM] * 3,
        out_specs=(VMEM, VMEM),
        name="finish",
    )(y, parts, base)


def per_device(n, side, anc_store, patterns, tile_counts, tile_owner, l_offdiag, diag_inverse):
    picked = pick_tiles(patterns.T, tile_counts, tile_owner, anc_store, l_offdiag, side)
    return finish(*level(*picked, diag_inverse, n))


def solution(mesh):
    in_specs = (
        P("snode", None),
        P(),
        P(),
        P(),
        P(("snode", "rows"), None),
        P(("snode", "rows"), None),
    )
    out_specs = (P(("snode", "rows"), None), P(("snode", "rows"), None))
    return jax.shard_map(
        functools.partial(per_device, mesh.shape["rows"], 8),
        mesh=mesh,
        in_specs=in_specs,
        out_specs=out_specs,
        check_vma=False,
    )
```

```python
import functools

import jax
import jax.numpy as jnp
from jax import lax
from jax.experimental import pallas as pl
from jax.experimental.pallas import tpu as pltpu
from jax.sharding import PartitionSpec as P

LANES = 128
MESH = pl.DeviceIdType.MESH
VMEM = pl.BlockSpec(memory_space=pltpu.VMEM)


ORDER = (1, 7, 2, 6, 3, 5, 4)
PARTS = 2


def pick_kernel(
    tile, patterns_ref, counts_ref, owner_ref, store_ref, l_ref,
    out_ref, src_ref, masked_ref, live_ref, sem,
):
    group, part = lax.axis_index("snode"), lax.axis_index("rows")
    majors, minors = out_ref.shape[:2]

    def start(i, carry):
        col = pl.multiple_of(patterns_ref[part, i] * tile, tile)
        pltpu.make_async_copy(
            store_ref.at[:, pl.ds(col, tile)], out_ref.at[i // minors, lax.rem(i, minors)], sem
        ).start()
        return carry

    lax.fori_loop(0, majors * minors, start, 0)
    slots = patterns_ref.shape[0]

    def look_up(i, carry):
        top = i * minors + lax.rem(group, minors)
        low = group // minors * minors + i
        for k in range(slots):
            src_ref[0, i * slots + k] = owner_ref[patterns_ref[k, top]]
            src_ref[1, i * slots + k] = owner_ref[patterns_ref[k, low]]
        return carry

    lax.fori_loop(0, majors, look_up, 0)
    live = (part < counts_ref[group]).astype(jnp.float32)
    keep = jnp.full(live_ref.shape, live, jnp.float32)
    live_ref[...] = keep
    loaded = l_ref[...]
    masked_ref[...] = jnp.where(keep > 0, loaded, jnp.zeros_like(loaded))
    pltpu.make_async_copy(out_ref, out_ref, sem).wait()


def pick_tiles(patterns, counts, owner, store, l_offdiag, side):
    tile = store.shape[0]
    smem = pl.BlockSpec(memory_space=pltpu.SMEM)
    return pl.pallas_call(
        functools.partial(pick_kernel, tile),
        out_shape=(
            jax.ShapeDtypeStruct((owner.shape[0] // side, side, tile, tile), store.dtype),
            jax.ShapeDtypeStruct((2, side * patterns.shape[0]), jnp.int32),
            jax.ShapeDtypeStruct(l_offdiag.shape, l_offdiag.dtype),
            jax.ShapeDtypeStruct((1, l_offdiag.shape[1]), jnp.float32),
        ),
        in_specs=[smem] * 3 + [pl.BlockSpec(memory_space=pl.ANY), VMEM],
        out_specs=(VMEM, smem, VMEM, VMEM),
        scratch_shapes=[pltpu.SemaphoreType.DMA],
        name="pick_tiles",
    )(patterns, counts, owner, store, l_offdiag)


def level_kernel(
    n, src_ref, out_tiles, l_ref, diag_ref, live_ref,
    y_ref, parts_ref, base_ref,
    top_mid, low_mid, held, sent, diag_all, u_all, stage, tiles, parts, wide, total,
    pool_send, pool_recv, chain_send, chain_recv, row_send, row_recv, local_sem,
):
    snode, me = lax.axis_index("snode"), lax.axis_index("rows")
    majors, minors, tile, _ = out_tiles.shape
    half = tile // 2
    major, minor = snode // minors, lax.rem(snode, minors)

    barrier = pltpu.get_barrier_semaphore()
    for step in range(1, n):
        pl.semaphore_signal(
            barrier, inc=1, device_id=(snode, lax.rem(me + step, n)), device_id_type=MESH
        )
    for step in ORDER:
        for peer in (
            major * minors + lax.rem(minor + step, minors),
            lax.rem(major + step, majors) * minors + minor,
        ):
            pl.semaphore_signal(barrier, inc=1, device_id=(peer, me), device_id_type=MESH)
    pl.semaphore_wait(barrier, n - 1 + 2 * len(ORDER))

    def row_copies(phase, src_of, dst):
        copies = []
        for step in range(1, n):
            peer = lax.rem(me + step, n)
            copy = pltpu.make_async_remote_copy(
                src_ref=src_of(peer),
                dst_ref=dst.at[me],
                send_sem=row_send.at[phase, step - 1],
                recv_sem=row_recv.at[phase, step - 1],
                device_id=(snode, peer),
                device_id_type=MESH,
            )
            copy.start()
            copies.append(copy)
        return copies

    def pool_copies():
        copies = []
        for step in ORDER:
            to_minor, to_major = lax.rem(minor + step, minors), lax.rem(major + step, majors)
            for lane, src, dst, device in (
                (0, top_out(to_minor), top_mid.at[minor], line(0, to_minor)),
                (1, low_out(to_major), low_mid.at[major], line(1, to_major)),
            ):
                copy = pltpu.make_async_remote_copy(
                    src_ref=src,
                    dst_ref=dst,
                    send_sem=pool_send.at[lane, step - 1],
                    recv_sem=pool_recv.at[lane, step - 1],
                    device_id=device,
                    device_id_type=MESH,
                )
                copy.start()
                copies.append(copy)
        return copies

    def line(lane, index):
        if lane == 0:
            return (major * minors + index, me)
        return (index * minors + minor, me)

    sign = 1 - 2 * lax.rem(me, 2)

    def own_part_of(lane, target, k):
        owner = src_ref[lane, target * n + k]
        if lane == 0:
            place, entry = owner // minors, lax.rem(owner, minors)
            return place, top_mid[entry, target]
        place, entry = lax.rem(owner, minors), owner // minors
        return place, low_mid[entry, target]

    def chain_step(lane, way, step, part, before):
        here, size = (major, majors) if lane == 0 else (minor, minors)
        length = size // 2 - way
        toward = sign if way else -sign
        target = lax.rem(here + toward * (length - step) + size, size)
        slots = range(part * n // PARTS, (part + 1) * n // PARTS)
        if before is not None:
            before.wait_recv()
        for k in slots:
            place, mine = own_part_of(lane, target, k)
            if before is not None:
                mine = jnp.where(place == here, mine, held[lane, way, step - 1, k])
            sent[lane, way, step, k] = mine
        span = pl.ds(part * n // PARTS, n // PARTS)
        copy = pltpu.make_async_remote_copy(
            src_ref=sent.at[lane, way, step, span],
            dst_ref=held.at[lane, way, step, span],
            send_sem=chain_send.at[lane, way, step, part],
            recv_sem=chain_recv.at[lane, way, step, part],
            device_id=line(1 - lane, lax.rem(here + toward + size, size)),
            device_id_type=MESH,
        )
        copy.start()
        return copy

    def local(slot, src, dst):
        copy = pltpu.make_async_copy(src, dst, local_sem.at[slot])
        copy.start()
        return copy

    top_out = lambda to: out_tiles.at[:, to, pl.ds(0, half)]
    low_out = lambda to: out_tiles.at[to, :, pl.ds(half, half)]
    diag_copies = row_copies(0, lambda peer: diag_ref, diag_all)
    first = pool_copies()
    own_diag = local(0, diag_ref, diag_all.at[me])
    own_top = local(1, top_out(minor), top_mid.at[minor])
    own_low = local(2, low_out(major), low_mid.at[major])
    own_diag.wait()
    for copy in diag_copies:
        copy.wait()

    band, width = diag_ref.shape
    depth = l_ref.shape[0]
    piece = diag_all[...].reshape(width, width)
    u_all[me] = jnp.dot(l_ref[...], piece, preferred_element_type=jnp.float32).astype(u_all.dtype)
    per_block = LANES // band
    start = pl.multiple_of(me // per_block * LANES, LANES)
    columns = diag_all[:, :, pl.ds(start, LANES)].reshape(width, LANES)
    wide[...] = lax.dot_general(
        columns, piece, (((0,), (0,)), ((), ())), preferred_element_type=jnp.float32
    )
    row = pl.multiple_of(lax.rem(me, per_block) * band, band)
    base_ref[...] = wide[pl.ds(row, band), :]
    u_copies = row_copies(1, lambda peer: u_all.at[me], u_all)
    own_top.wait()
    own_low.wait()
    for copy in first:
        copy.wait()
    last, everything = {}, []
    for step in range(max(majors, minors) // 2):
        for part in range(PARTS):
            for way in (0, 1):
                for lane in (0, 1):
                    if step < (majors, minors)[lane] // 2 - way:
                        key = (lane, way, part)
                        last[key] = chain_step(lane, way, step, part, last.get(key))
                        everything.append(last[key])
    for copy in u_copies:
        copy.wait()
    for copy in last.values():
        copy.wait_recv()
    for lane in (0, 1):
        here, size = (major, majors) if lane == 0 else (minor, minors)
        for k in range(n):
            place, mine = own_part_of(lane, here, k)
            away = lax.rem((place - here) * sign + size, size)
            other = jnp.where(
                away <= size // 2,
                held[lane, 0, size // 2 - 1, k],
                held[lane, 1, size // 2 - 2, k],
            )
            stage[k, lane * half : (lane + 1) * half] = jnp.where(away == 0, mine, other)
    for copy in everything:
        copy.wait_send()
    tile_copies = row_copies(2, lambda peer: stage.at[peer], tiles)
    total[...] = jnp.dot(stage[me], u_all[me], preferred_element_type=jnp.float32)
    for step, copy in enumerate(tile_copies):
        copy.wait()
        origin = lax.rem(me + n - 1 - step, n)
        total[...] += jnp.dot(tiles[origin], u_all[origin], preferred_element_type=jnp.float32)
    y = (-(total[...] * live_ref[...])).astype(y_ref.dtype)
    part = lax.dot_general(
        u_all[me], y, (((0,), (0,)), ((), ())), preferred_element_type=jnp.float32
    )
    parts[...] = part.astype(parts.dtype).reshape(parts.shape)
    y_ref[...] = y
    part_copies = row_copies(3, lambda peer: parts.at[peer], parts_ref)
    local(5, parts.at[me], parts_ref.at[me]).wait()
    for copy in part_copies:
        copy.wait()


def level(outgoing, sources, masked_l, live, diag, n):
    majors, minors, tile, _ = outgoing.shape
    band, width = diag.shape
    bf16 = jnp.bfloat16
    return pl.pallas_call(
        functools.partial(level_kernel, n),
        out_shape=(
            jax.ShapeDtypeStruct((tile, width), bf16),
            jax.ShapeDtypeStruct((n, band, width), bf16),
            jax.ShapeDtypeStruct((band, width), jnp.float32),
        ),
        in_specs=[pl.BlockSpec(memory_space=pltpu.SMEM)] + [VMEM] * 4,
        out_specs=(VMEM,) * 3,
        scratch_shapes=[
            pltpu.VMEM((minors, majors, tile // 2, tile), bf16),
            pltpu.VMEM((majors, minors, tile // 2, tile), bf16),
            pltpu.VMEM((2, 2, max(majors, minors) // 2, n, tile // 2, tile), bf16),
            pltpu.VMEM((2, 2, max(majors, minors) // 2, n, tile // 2, tile), bf16),
            pltpu.VMEM((n, band, width), bf16),
            pltpu.VMEM((n, tile, width), bf16),
            pltpu.VMEM((n, tile, tile), bf16),
            pltpu.VMEM((n, tile, tile), bf16),
            pltpu.VMEM((n, band, width), bf16),
            pltpu.VMEM((LANES, width), jnp.float32),
            pltpu.VMEM((tile, width), jnp.float32),
            pltpu.SemaphoreType.DMA((2, len(ORDER))),
            pltpu.SemaphoreType.DMA((2, len(ORDER))),
            pltpu.SemaphoreType.DMA((2, 2, max(majors, minors) // 2, PARTS)),
            pltpu.SemaphoreType.DMA((2, 2, max(majors, minors) // 2, PARTS)),
            pltpu.SemaphoreType.DMA((4, n - 1)),
            pltpu.SemaphoreType.DMA((4, n - 1)),
            pltpu.SemaphoreType.DMA((6,)),
        ],
        compiler_params=pltpu.CompilerParams(collective_id=1, has_side_effects=True),
        name="level",
    )(sources, outgoing, masked_l, diag, live)


def finish_kernel(y_ref, parts_ref, base_ref, off_ref, diag_ref):
    off_ref[...] = y_ref[...]
    total = base_ref[...]
    for m in range(parts_ref.shape[0]):
        total -= parts_ref[m].astype(jnp.float32)
    diag_ref[...] = total


def finish(y, parts, base):
    return pl.pallas_call(
        finish_kernel,
        out_shape=(
            jax.ShapeDtypeStruct(y.shape, y.dtype),
            jax.ShapeDtypeStruct(base.shape, base.dtype),
        ),
        in_specs=[VMEM] * 3,
        out_specs=(VMEM, VMEM),
        name="finish",
    )(y, parts, base)


def per_device(n, side, anc_store, patterns, tile_counts, tile_owner, l_offdiag, diag_inverse):
    picked = pick_tiles(patterns.T, tile_counts, tile_owner, anc_store, l_offdiag, side)
    return finish(*level(*picked, diag_inverse, n))


def solution(mesh):
    in_specs = (
        P("snode", None),
        P(),
        P(),
        P(),
        P(("snode", "rows"), None),
        P(("snode", "rows"), None),
    )
    out_specs = (P(("snode", "rows"), None), P(("snode", "rows"), None))
    return jax.shard_map(
        functools.partial(per_device, mesh.shape["rows"], 8),
        mesh=mesh,
        in_specs=in_specs,
        out_specs=out_specs,
        check_vma=False,
    )
```

```python
import functools

import jax
import jax.numpy as jnp
from jax import lax
from jax.experimental import pallas as pl
from jax.experimental.pallas import tpu as pltpu
from jax.sharding import PartitionSpec as P

LANES = 128
MESH = pl.DeviceIdType.MESH
VMEM = pl.BlockSpec(memory_space=pltpu.VMEM)


ORDER = (1, 7, 2, 6, 3, 5, 4)
PARTS = 2


def pick_kernel(
    tile, patterns_ref, counts_ref, owner_ref, store_ref, l_ref,
    out_ref, src_ref, masked_ref, live_ref, sem,
):
    group, part = lax.axis_index("snode"), lax.axis_index("rows")
    majors, minors = out_ref.shape[:2]

    def start(i, carry):
        col = pl.multiple_of(patterns_ref[part, i] * tile, tile)
        pltpu.make_async_copy(
            store_ref.at[:, pl.ds(col, tile)], out_ref.at[i // minors, lax.rem(i, minors)], sem
        ).start()
        return carry

    lax.fori_loop(0, majors * minors, start, 0)
    slots = patterns_ref.shape[0]

    def look_up(i, carry):
        top = i * minors + lax.rem(group, minors)
        low = group // minors * minors + i
        for k in range(slots):
            src_ref[0, i * slots + k] = owner_ref[patterns_ref[k, top]]
            src_ref[1, i * slots + k] = owner_ref[patterns_ref[k, low]]
        return carry

    lax.fori_loop(0, majors, look_up, 0)
    live = (part < counts_ref[group]).astype(jnp.float32)
    keep = jnp.full(live_ref.shape, live, jnp.float32)
    live_ref[...] = keep
    loaded = l_ref[...]
    masked_ref[...] = jnp.where(keep > 0, loaded, jnp.zeros_like(loaded))
    pltpu.make_async_copy(out_ref, out_ref, sem).wait()


def pick_tiles(patterns, counts, owner, store, l_offdiag, side):
    tile = store.shape[0]
    smem = pl.BlockSpec(memory_space=pltpu.SMEM)
    return pl.pallas_call(
        functools.partial(pick_kernel, tile),
        out_shape=(
            jax.ShapeDtypeStruct((owner.shape[0] // side, side, tile, tile), store.dtype),
            jax.ShapeDtypeStruct((2, side * patterns.shape[0]), jnp.int32),
            jax.ShapeDtypeStruct(l_offdiag.shape, l_offdiag.dtype),
            jax.ShapeDtypeStruct((1, l_offdiag.shape[1]), jnp.float32),
        ),
        in_specs=[smem] * 3 + [pl.BlockSpec(memory_space=pl.ANY), VMEM],
        out_specs=(VMEM, smem, VMEM, VMEM),
        scratch_shapes=[pltpu.SemaphoreType.DMA],
        name="pick_tiles",
    )(patterns, counts, owner, store, l_offdiag)


def level_kernel(
    n, src_ref, out_tiles, l_ref, diag_ref, live_ref,
    y_ref, parts_ref, base_ref,
    top_mid, low_mid, held, sent, diag_all, u_all, stage, tiles, parts, wide, total,
    pool_send, pool_recv, chain_send, chain_recv, row_send, row_recv, local_sem,
):
    snode, me = lax.axis_index("snode"), lax.axis_index("rows")
    majors, minors, tile, _ = out_tiles.shape
    half = tile // 2
    major, minor = snode // minors, lax.rem(snode, minors)

    barrier = pltpu.get_barrier_semaphore()
    for step in range(1, n):
        pl.semaphore_signal(
            barrier, inc=1, device_id=(snode, lax.rem(me + step, n)), device_id_type=MESH
        )
    for step in ORDER:
        for peer in (
            major * minors + lax.rem(minor + step, minors),
            lax.rem(major + step, majors) * minors + minor,
        ):
            pl.semaphore_signal(barrier, inc=1, device_id=(peer, me), device_id_type=MESH)
    pl.semaphore_wait(barrier, n - 1 + 2 * len(ORDER))

    def row_copies(phase, src_of, dst):
        copies = []
        for step in range(1, n):
            peer = lax.rem(me + step, n)
            copy = pltpu.make_async_remote_copy(
                src_ref=src_of(peer),
                dst_ref=dst.at[me],
                send_sem=row_send.at[phase, step - 1],
                recv_sem=row_recv.at[phase, step - 1],
                device_id=(snode, peer),
                device_id_type=MESH,
            )
            copy.start()
            copies.append(copy)
        return copies

    def pool_copies():
        copies = []
        for step in ORDER:
            to_minor = lax.rem(minor + sign * step + minors, minors)
            to_major = lax.rem(major + sign * step + majors, majors)
            for lane, src, dst, device in (
                (0, top_out(to_minor), top_mid.at[minor], line(0, to_minor)),
                (1, low_out(to_major), low_mid.at[major], line(1, to_major)),
            ):
                copy = pltpu.make_async_remote_copy(
                    src_ref=src,
                    dst_ref=dst,
                    send_sem=pool_send.at[lane, step - 1],
                    recv_sem=pool_recv.at[lane, step - 1],
                    device_id=device,
                    device_id_type=MESH,
                )
                copy.start()
                copies.append(copy)
        return copies

    def line(lane, index):
        if lane == 0:
            return (major * minors + index, me)
        return (index * minors + minor, me)

    sign = 1 - 2 * lax.rem(me, 2)

    def own_part_of(lane, target, k):
        owner = src_ref[lane, target * n + k]
        if lane == 0:
            place, entry = owner // minors, lax.rem(owner, minors)
            return place, top_mid[entry, target]
        place, entry = lax.rem(owner, minors), owner // minors
        return place, low_mid[entry, target]

    def chain_step(lane, way, step, part, before):
        here, size = (major, majors) if lane == 0 else (minor, minors)
        length = size // 2 - way
        toward = sign if way else -sign
        target = lax.rem(here + toward * (length - step) + size, size)
        slots = range(part * n // PARTS, (part + 1) * n // PARTS)
        if before is not None:
            before.wait_recv()
        for k in slots:
            place, mine = own_part_of(lane, target, k)
            if before is not None:
                mine = jnp.where(place == here, mine, held[lane, way, step - 1, k])
            sent[lane, way, step, k] = mine
        span = pl.ds(part * n // PARTS, n // PARTS)
        copy = pltpu.make_async_remote_copy(
            src_ref=sent.at[lane, way, step, span],
            dst_ref=held.at[lane, way, step, span],
            send_sem=chain_send.at[lane, way, step, part],
            recv_sem=chain_recv.at[lane, way, step, part],
            device_id=line(1 - lane, lax.rem(here + toward + size, size)),
            device_id_type=MESH,
        )
        copy.start()
        return copy

    def local(slot, src, dst):
        copy = pltpu.make_async_copy(src, dst, local_sem.at[slot])
        copy.start()
        return copy

    top_out = lambda to: out_tiles.at[:, to, pl.ds(0, half)]
    low_out = lambda to: out_tiles.at[to, :, pl.ds(half, half)]
    diag_copies = row_copies(0, lambda peer: diag_ref, diag_all)
    first = pool_copies()
    own_diag = local(0, diag_ref, diag_all.at[me])
    own_top = local(1, top_out(minor), top_mid.at[minor])
    own_low = local(2, low_out(major), low_mid.at[major])
    own_diag.wait()
    for copy in diag_copies:
        copy.wait()

    band, width = diag_ref.shape
    depth = l_ref.shape[0]
    piece = diag_all[...].reshape(width, width)
    u_all[me] = jnp.dot(l_ref[...], piece, preferred_element_type=jnp.float32).astype(u_all.dtype)
    per_block = LANES // band
    start = pl.multiple_of(me // per_block * LANES, LANES)
    columns = diag_all[:, :, pl.ds(start, LANES)].reshape(width, LANES)
    wide[...] = lax.dot_general(
        columns, piece, (((0,), (0,)), ((), ())), preferred_element_type=jnp.float32
    )
    row = pl.multiple_of(lax.rem(me, per_block) * band, band)
    base_ref[...] = wide[pl.ds(row, band), :]
    u_copies = row_copies(1, lambda peer: u_all.at[me], u_all)
    own_top.wait()
    own_low.wait()
    for copy in first:
        copy.wait_recv()
    last, everything = {}, []
    for step in range(max(majors, minors) // 2):
        for part in range(PARTS):
            for way in (0, 1):
                for lane in (0, 1):
                    if step < (majors, minors)[lane] // 2 - way:
                        key = (lane, way, part)
                        last[key] = chain_step(lane, way, step, part, last.get(key))
                        everything.append(last[key])
    for copy in u_copies:
        copy.wait()
    for copy in last.values():
        copy.wait_recv()
    for lane in (0, 1):
        here, size = (major, majors) if lane == 0 else (minor, minors)
        for k in range(n):
            place, mine = own_part_of(lane, here, k)
            away = lax.rem((place - here) * sign + size, size)
            other = jnp.where(
                away <= size // 2,
                held[lane, 0, size // 2 - 1, k],
                held[lane, 1, size // 2 - 2, k],
            )
            stage[k, lane * half : (lane + 1) * half] = jnp.where(away == 0, mine, other)
    tile_copies = row_copies(2, lambda peer: stage.at[peer], tiles)
    total[...] = jnp.dot(stage[me], u_all[me], preferred_element_type=jnp.float32)
    for step, copy in enumerate(tile_copies):
        copy.wait()
        origin = lax.rem(me + n - 1 - step, n)
        total[...] += jnp.dot(tiles[origin], u_all[origin], preferred_element_type=jnp.float32)
    y = (-(total[...] * live_ref[...])).astype(y_ref.dtype)
    part = lax.dot_general(
        u_all[me], y, (((0,), (0,)), ((), ())), preferred_element_type=jnp.float32
    )
    parts[...] = part.astype(parts.dtype).reshape(parts.shape)
    y_ref[...] = y
    part_copies = row_copies(3, lambda peer: parts.at[peer], parts_ref)
    local(5, parts.at[me], parts_ref.at[me]).wait()
    for copy in part_copies:
        copy.wait_recv()
    for copy in first + everything + part_copies:
        copy.wait_send()


def level(outgoing, sources, masked_l, live, diag, n):
    majors, minors, tile, _ = outgoing.shape
    band, width = diag.shape
    bf16 = jnp.bfloat16
    return pl.pallas_call(
        functools.partial(level_kernel, n),
        out_shape=(
            jax.ShapeDtypeStruct((tile, width), bf16),
            jax.ShapeDtypeStruct((n, band, width), bf16),
            jax.ShapeDtypeStruct((band, width), jnp.float32),
        ),
        in_specs=[
            pl.BlockSpec(memory_space=pltpu.SMEM),
            pl.BlockSpec(memory_space=pl.ANY),
        ]
        + [VMEM] * 3,
        out_specs=(VMEM,) * 3,
        scratch_shapes=[
            pltpu.VMEM((minors, majors, tile // 2, tile), bf16),
            pltpu.VMEM((majors, minors, tile // 2, tile), bf16),
            pltpu.VMEM((2, 2, max(majors, minors) // 2, n, tile // 2, tile), bf16),
            pltpu.VMEM((2, 2, max(majors, minors) // 2, n, tile // 2, tile), bf16),
            pltpu.VMEM((n, band, width), bf16),
            pltpu.VMEM((n, tile, width), bf16),
            pltpu.VMEM((n, tile, tile), bf16),
            pltpu.VMEM((n, tile, tile), bf16),
            pltpu.VMEM((n, band, width), bf16),
            pltpu.VMEM((LANES, width), jnp.float32),
            pltpu.VMEM((tile, width), jnp.float32),
            pltpu.SemaphoreType.DMA((2, len(ORDER))),
            pltpu.SemaphoreType.DMA((2, len(ORDER))),
            pltpu.SemaphoreType.DMA((2, 2, max(majors, minors) // 2, PARTS)),
            pltpu.SemaphoreType.DMA((2, 2, max(majors, minors) // 2, PARTS)),
            pltpu.SemaphoreType.DMA((4, n - 1)),
            pltpu.SemaphoreType.DMA((4, n - 1)),
            pltpu.SemaphoreType.DMA((6,)),
        ],
        compiler_params=pltpu.CompilerParams(collective_id=1, has_side_effects=True),
        name="level",
    )(sources, outgoing, masked_l, diag, live)


def finish_kernel(y_ref, parts_ref, base_ref, off_ref, diag_ref):
    off_ref[...] = y_ref[...]
    total = base_ref[...]
    for m in range(parts_ref.shape[0]):
        total -= parts_ref[m].astype(jnp.float32)
    diag_ref[...] = total


def finish(y, parts, base):
    return pl.pallas_call(
        finish_kernel,
        out_shape=(
            jax.ShapeDtypeStruct(y.shape, y.dtype),
            jax.ShapeDtypeStruct(base.shape, base.dtype),
        ),
        in_specs=[VMEM] * 3,
        out_specs=(VMEM, VMEM),
        name="finish",
    )(y, parts, base)


def per_device(n, side, anc_store, patterns, tile_counts, tile_owner, l_offdiag, diag_inverse):
    picked = pick_tiles(patterns.T, tile_counts, tile_owner, anc_store, l_offdiag, side)
    return finish(*level(*picked, diag_inverse, n))


def solution(mesh):
    in_specs = (
        P("snode", None),
        P(),
        P(),
        P(),
        P(("snode", "rows"), None),
        P(("snode", "rows"), None),
    )
    out_specs = (P(("snode", "rows"), None), P(("snode", "rows"), None))
    return jax.shard_map(
        functools.partial(per_device, mesh.shape["rows"], 8),
        mesh=mesh,
        in_specs=in_specs,
        out_specs=out_specs,
        check_vma=False,
    )
```

```python
import functools

import jax
import jax.numpy as jnp
from jax import lax
from jax.experimental import pallas as pl
from jax.experimental.pallas import tpu as pltpu
from jax.sharding import PartitionSpec as P

LANES = 128
MESH = pl.DeviceIdType.MESH
VMEM = pl.BlockSpec(memory_space=pltpu.VMEM)


ORDER = (1, 7, 2, 6, 3, 5, 4)
PARTS = 2


def pick_kernel(
    tile, patterns_ref, counts_ref, owner_ref, store_ref, l_ref,
    out_ref, src_ref, masked_ref, live_ref, sem,
):
    group, part = lax.axis_index("snode"), lax.axis_index("rows")
    majors, minors = out_ref.shape[:2]

    def start(i, carry):
        col = pl.multiple_of(patterns_ref[part, i] * tile, tile)
        pltpu.make_async_copy(
            store_ref.at[:, pl.ds(col, tile)], out_ref.at[i // minors, lax.rem(i, minors)], sem
        ).start()
        return carry

    lax.fori_loop(0, majors * minors, start, 0)
    slots = patterns_ref.shape[0]

    def look_up(i, carry):
        top = i * minors + lax.rem(group, minors)
        low = group // minors * minors + i
        for k in range(slots):
            src_ref[0, i * slots + k] = owner_ref[patterns_ref[k, top]]
            src_ref[1, i * slots + k] = owner_ref[patterns_ref[k, low]]
        return carry

    lax.fori_loop(0, majors, look_up, 0)
    live = (part < counts_ref[group]).astype(jnp.float32)
    keep = jnp.full(live_ref.shape, live, jnp.float32)
    live_ref[...] = keep
    loaded = l_ref[...]
    masked_ref[...] = jnp.where(keep > 0, loaded, jnp.zeros_like(loaded))
    pltpu.make_async_copy(out_ref, out_ref, sem).wait()


def pick_tiles(patterns, counts, owner, store, l_offdiag, side):
    tile = store.shape[0]
    smem = pl.BlockSpec(memory_space=pltpu.SMEM)
    return pl.pallas_call(
        functools.partial(pick_kernel, tile),
        out_shape=(
            jax.ShapeDtypeStruct((owner.shape[0] // side, side, tile, tile), store.dtype),
            jax.ShapeDtypeStruct((2, side * patterns.shape[0]), jnp.int32),
            jax.ShapeDtypeStruct(l_offdiag.shape, l_offdiag.dtype),
            jax.ShapeDtypeStruct((1, l_offdiag.shape[1]), jnp.float32),
        ),
        in_specs=[smem] * 3 + [pl.BlockSpec(memory_space=pl.ANY), VMEM],
        out_specs=(VMEM, smem, VMEM, VMEM),
        scratch_shapes=[pltpu.SemaphoreType.DMA],
        name="pick_tiles",
    )(patterns, counts, owner, store, l_offdiag)


def level_kernel(
    n, src_ref, out_tiles, l_ref, diag_ref, live_ref,
    y_ref, parts_ref, base_ref,
    top_mid, low_mid, held, sent, diag_all, u_all, stage, tiles, parts, wide, total,
    pool_send, pool_recv, chain_send, chain_recv, row_send, row_recv, local_sem,
):
    snode, me = lax.axis_index("snode"), lax.axis_index("rows")
    majors, minors, tile, _ = out_tiles.shape
    half = tile // 2
    major, minor = snode // minors, lax.rem(snode, minors)

    barrier = pltpu.get_barrier_semaphore()
    for step in range(1, n):
        pl.semaphore_signal(
            barrier, inc=1, device_id=(snode, lax.rem(me + step, n)), device_id_type=MESH
        )
    for step in ORDER:
        for peer in (
            major * minors + lax.rem(minor + step, minors),
            lax.rem(major + step, majors) * minors + minor,
        ):
            pl.semaphore_signal(barrier, inc=1, device_id=(peer, me), device_id_type=MESH)
    pl.semaphore_wait(barrier, n - 1 + 2 * len(ORDER))

    far_first = sorted(range(1, n), key=lambda step: (abs(step - n // 2), step))

    def row_copies(phase, src_of, dst):
        copies = []
        for step in far_first:
            peer = lax.rem(me + step, n)
            copy = pltpu.make_async_remote_copy(
                src_ref=src_of(peer),
                dst_ref=dst.at[me],
                send_sem=row_send.at[phase, step - 1],
                recv_sem=row_recv.at[phase, step - 1],
                device_id=(snode, peer),
                device_id_type=MESH,
            )
            copy.start()
            copies.append(copy)
        return copies

    def pool_copies():
        copies = []
        for step in ORDER:
            to_minor = lax.rem(minor + sign * step + minors, minors)
            to_major = lax.rem(major + sign * step + majors, majors)
            for lane, src, dst, device in (
                (0, top_out(to_minor), top_mid.at[minor], line(0, to_minor)),
                (1, low_out(to_major), low_mid.at[major], line(1, to_major)),
            ):
                copy = pltpu.make_async_remote_copy(
                    src_ref=src,
                    dst_ref=dst,
                    send_sem=pool_send.at[lane, step - 1],
                    recv_sem=pool_recv.at[lane, step - 1],
                    device_id=device,
                    device_id_type=MESH,
                )
                copy.start()
                copies.append(copy)
        return copies

    def line(lane, index):
        if lane == 0:
            return (major * minors + index, me)
        return (index * minors + minor, me)

    sign = 1 - 2 * lax.rem(me, 2)

    def own_part_of(lane, target, k):
        owner = src_ref[lane, target * n + k]
        if lane == 0:
            place, entry = owner // minors, lax.rem(owner, minors)
            return place, top_mid[entry, target]
        place, entry = lax.rem(owner, minors), owner // minors
        return place, low_mid[entry, target]

    def chain_step(lane, way, step, part, before):
        here, size = (major, majors) if lane == 0 else (minor, minors)
        length = size // 2 - way
        toward = sign if way else -sign
        target = lax.rem(here + toward * (length - step) + size, size)
        slots = range(part * n // PARTS, (part + 1) * n // PARTS)
        if before is not None:
            before.wait_recv()
        for k in slots:
            place, mine = own_part_of(lane, target, k)
            if before is not None:
                mine = jnp.where(place == here, mine, held[lane, way, step - 1, k])
            sent[lane, way, step, k] = mine
        span = pl.ds(part * n // PARTS, n // PARTS)
        copy = pltpu.make_async_remote_copy(
            src_ref=sent.at[lane, way, step, span],
            dst_ref=held.at[lane, way, step, span],
            send_sem=chain_send.at[lane, way, step, part],
            recv_sem=chain_recv.at[lane, way, step, part],
            device_id=line(1 - lane, lax.rem(here + toward + size, size)),
            device_id_type=MESH,
        )
        copy.start()
        return copy

    def local(slot, src, dst):
        copy = pltpu.make_async_copy(src, dst, local_sem.at[slot])
        copy.start()
        return copy

    top_out = lambda to: out_tiles.at[:, to, pl.ds(0, half)]
    low_out = lambda to: out_tiles.at[to, :, pl.ds(half, half)]
    diag_copies = row_copies(0, lambda peer: diag_ref, diag_all)
    first = pool_copies()
    own_diag = local(0, diag_ref, diag_all.at[me])
    own_top = local(1, top_out(minor), top_mid.at[minor])
    own_low = local(2, low_out(major), low_mid.at[major])
    own_diag.wait()
    for copy in diag_copies:
        copy.wait()

    band, width = diag_ref.shape
    depth = l_ref.shape[0]
    piece = diag_all[...].reshape(width, width)
    u_all[me] = jnp.dot(l_ref[...], piece, preferred_element_type=jnp.float32).astype(u_all.dtype)
    per_block = LANES // band
    start = pl.multiple_of(me // per_block * LANES, LANES)
    columns = diag_all[:, :, pl.ds(start, LANES)].reshape(width, LANES)
    wide[...] = lax.dot_general(
        columns, piece, (((0,), (0,)), ((), ())), preferred_element_type=jnp.float32
    )
    row = pl.multiple_of(lax.rem(me, per_block) * band, band)
    base_ref[...] = wide[pl.ds(row, band), :]
    u_copies = row_copies(1, lambda peer: u_all.at[me], u_all)
    own_top.wait()
    own_low.wait()
    for copy in first:
        copy.wait_recv()
    last, everything = {}, []
    for step in range(max(majors, minors) // 2):
        for part in range(PARTS):
            for way in (0, 1):
                for lane in (0, 1):
                    if step < (majors, minors)[lane] // 2 - way:
                        key = (lane, way, part)
                        last[key] = chain_step(lane, way, step, part, last.get(key))
                        everything.append(last[key])
    for copy in u_copies:
        copy.wait()
    for copy in last.values():
        copy.wait_recv()
    for lane in (0, 1):
        here, size = (major, majors) if lane == 0 else (minor, minors)
        for k in range(n):
            place, mine = own_part_of(lane, here, k)
            away = lax.rem((place - here) * sign + size, size)
            other = jnp.where(
                away <= size // 2,
                held[lane, 0, size // 2 - 1, k],
                held[lane, 1, size // 2 - 2, k],
            )
            stage[k, lane * half : (lane + 1) * half] = jnp.where(away == 0, mine, other)
    tile_copies = row_copies(2, lambda peer: stage.at[peer], tiles)
    total[...] = jnp.dot(stage[me], u_all[me], preferred_element_type=jnp.float32)
    for step, copy in reversed(list(zip(far_first, tile_copies))):
        copy.wait()
        origin = lax.rem(me + n - step, n)
        total[...] += jnp.dot(tiles[origin], u_all[origin], preferred_element_type=jnp.float32)
    y = (-(total[...] * live_ref[...])).astype(y_ref.dtype)
    part = lax.dot_general(
        u_all[me], y, (((0,), (0,)), ((), ())), preferred_element_type=jnp.float32
    )
    parts[...] = part.astype(parts.dtype).reshape(parts.shape)
    y_ref[...] = y
    part_copies = row_copies(3, lambda peer: parts.at[peer], parts_ref)
    local(5, parts.at[me], parts_ref.at[me]).wait()
    for copy in part_copies:
        copy.wait_recv()
    for copy in first + everything + part_copies:
        copy.wait_send()


def level(outgoing, sources, masked_l, live, diag, n):
    majors, minors, tile, _ = outgoing.shape
    band, width = diag.shape
    bf16 = jnp.bfloat16
    return pl.pallas_call(
        functools.partial(level_kernel, n),
        out_shape=(
            jax.ShapeDtypeStruct((tile, width), bf16),
            jax.ShapeDtypeStruct((n, band, width), bf16),
            jax.ShapeDtypeStruct((band, width), jnp.float32),
        ),
        in_specs=[
            pl.BlockSpec(memory_space=pltpu.SMEM),
            pl.BlockSpec(memory_space=pl.ANY),
        ]
        + [VMEM] * 3,
        out_specs=(VMEM,) * 3,
        scratch_shapes=[
            pltpu.VMEM((minors, majors, tile // 2, tile), bf16),
            pltpu.VMEM((majors, minors, tile // 2, tile), bf16),
            pltpu.VMEM((2, 2, max(majors, minors) // 2, n, tile // 2, tile), bf16),
            pltpu.VMEM((2, 2, max(majors, minors) // 2, n, tile // 2, tile), bf16),
            pltpu.VMEM((n, band, width), bf16),
            pltpu.VMEM((n, tile, width), bf16),
            pltpu.VMEM((n, tile, tile), bf16),
            pltpu.VMEM((n, tile, tile), bf16),
            pltpu.VMEM((n, band, width), bf16),
            pltpu.VMEM((LANES, width), jnp.float32),
            pltpu.VMEM((tile, width), jnp.float32),
            pltpu.SemaphoreType.DMA((2, len(ORDER))),
            pltpu.SemaphoreType.DMA((2, len(ORDER))),
            pltpu.SemaphoreType.DMA((2, 2, max(majors, minors) // 2, PARTS)),
            pltpu.SemaphoreType.DMA((2, 2, max(majors, minors) // 2, PARTS)),
            pltpu.SemaphoreType.DMA((4, n - 1)),
            pltpu.SemaphoreType.DMA((4, n - 1)),
            pltpu.SemaphoreType.DMA((6,)),
        ],
        compiler_params=pltpu.CompilerParams(collective_id=1, has_side_effects=True),
        name="level",
    )(sources, outgoing, masked_l, diag, live)


def finish_kernel(y_ref, parts_ref, base_ref, off_ref, diag_ref):
    off_ref[...] = y_ref[...]
    total = base_ref[...]
    for m in range(parts_ref.shape[0]):
        total -= parts_ref[m].astype(jnp.float32)
    diag_ref[...] = total


def finish(y, parts, base):
    return pl.pallas_call(
        finish_kernel,
        out_shape=(
            jax.ShapeDtypeStruct(y.shape, y.dtype),
            jax.ShapeDtypeStruct(base.shape, base.dtype),
        ),
        in_specs=[VMEM] * 3,
        out_specs=(VMEM, VMEM),
        name="finish",
    )(y, parts, base)


def per_device(n, side, anc_store, patterns, tile_counts, tile_owner, l_offdiag, diag_inverse):
    picked = pick_tiles(patterns.T, tile_counts, tile_owner, anc_store, l_offdiag, side)
    return finish(*level(*picked, diag_inverse, n))


def solution(mesh):
    in_specs = (
        P("snode", None),
        P(),
        P(),
        P(),
        P(("snode", "rows"), None),
        P(("snode", "rows"), None),
    )
    out_specs = (P(("snode", "rows"), None), P(("snode", "rows"), None))
    return jax.shard_map(
        functools.partial(per_device, mesh.shape["rows"], 8),
        mesh=mesh,
        in_specs=in_specs,
        out_specs=out_specs,
        check_vma=False,
    )
```
